32 devices in a mesh: frag: 4 (over y, x), tile: 4 (over z), ka: 2 (over core).
Axes of the slice: x: 2, y: 2, z: 4, core: 2. Of those that a mesh axis runs over, the one named last changes fastest.
Arguments:
- sizes: int32 [32], replicated, may hold values from 40 to 400
- neighbors: int32 [32, 4], P('frag'), may hold values from 0 to 31, as said below
- slot_fragment: int32 [32], replicated, may hold values from 0 to 31, as said below
- density: bfloat16 [32, 512, 512], P('frag', ('tile', 'ka')), may hold values from -6 to 6
- hcore: bfloat16 [32, 512, 512], P('frag', ('tile', 'ka')), may hold values from -3 to 3
- integrals: bfloat16 [32, 16, 512, 512], P('frag', ('tile', 'ka')), may hold values from -0.15625 to 0.15625
- couple: bfloat16 [32, 4, 512, 512], P('frag', None, ('tile', 'ka')), may hold values from -2.390625 to 2.390625
Outputs:
- fock: float32 [32, 512, 512], P('frag', ('tile', 'ka'))
The draws below stay inside these ranges and needn't reach their ends.
Inputs may be any that keep to these rules, and one draw needn't show every extreme that they name: `neighbors`: fragment f belongs to group f // 8; each entry names a fragment other than f itself, belonging to the same group or to the next group on either side. `slot_fragment`: A permutation of the fragments; slots s with s // 8 == h form balanced group h; no group's fragments fill more than 2 slots of one balanced group, and some pair of groups reaches 2.
All inputs are finite; a program needn't handle non-finite values.
Results may differ from the reference program's by a relative error of at most 0.002.
Values may be sent and summed in bfloat16 or wider, within the bound.
A program may use at most 64 MiB of HBM per device.

```python
import jax
import jax.numpy as jnp
from jax import lax

TILE = 128
NB = 512
FPG = 8
NFRAG = 32
CHOL = 16
NNB = 4
N_FRAG = 4


def draw_layout(key):
    base = jax.random.fold_in(key, 11)
    keys = jax.random.split(base, 8)
    fragments = jnp.arange(NFRAG, dtype=jnp.int32)
    owner_group = fragments // FPG
    peptide = jax.random.randint(keys[0], (N_FRAG,), 0, 10) < 3
    chosen = jax.random.randint(keys[1], (), 0, N_FRAG)
    peptide = peptide | (jnp.arange(N_FRAG) == chosen)
    water_size = jax.random.randint(keys[2], (NFRAG,), TILE * 5 // 16, TILE + 1)
    peptide_size = jax.random.randint(keys[3], (NFRAG,), TILE * 3 // 2, NB * 25 // 32 + 1)
    frag_sizes = jnp.where(peptide[owner_group], peptide_size, water_size).astype(jnp.int32)
    scores = (frag_sizes * FPG + fragments % FPG).reshape(N_FRAG, FPG)
    rank_order = jnp.argsort(-scores, axis=1, stable=True).astype(jnp.int32)
    offset_perm = jax.random.permutation(keys[4], N_FRAG).astype(jnp.int32)
    offsets = offset_perm[jnp.arange(FPG) % N_FRAG]
    group_perm = jax.random.permutation(keys[5], N_FRAG).astype(jnp.int32)
    other_perm = jax.random.permutation(keys[6], N_FRAG).astype(jnp.int32)
    group_inv = jnp.argsort(group_perm).astype(jnp.int32)
    other_inv = jnp.argsort(other_perm).astype(jnp.int32)
    source = group_inv[(other_inv[:, None] - offsets[None, :]) % N_FRAG]
    ranks = jnp.broadcast_to(jnp.arange(FPG, dtype=jnp.int32)[None, :], (N_FRAG, FPG))
    placed = source * FPG + rank_order[source, ranks]
    shuffle = jax.random.randint(keys[7], (N_FRAG, FPG), 0, 1 << 20) * FPG + ranks
    slot_perm = jnp.argsort(shuffle, axis=1, stable=True).astype(jnp.int32)
    slots = jnp.take_along_axis(placed, slot_perm, axis=1).reshape(NFRAG).astype(jnp.int32)
    return (frag_sizes, slots)


def draw_sizes(key, part):
    return draw_layout(key)[0]


def draw_slot_fragment(key, part):
    return draw_layout(key)[1]


def draw_neighbors(key, part):
    base = jax.random.fold_in(key, 23)
    keys = jax.random.split(base, 3)
    fragments = jnp.arange(NFRAG, dtype=jnp.int32)
    owner_group = fragments // FPG
    group_step = jax.random.randint(keys[0], (NFRAG, NNB), -1, 2)
    near_group = owner_group[:, None] + group_step
    near_group = jnp.where(near_group < 0, 1, near_group)
    near_group = jnp.where(near_group >= N_FRAG, N_FRAG - 2, near_group)
    local_shift = jax.random.randint(keys[1], (NFRAG, NNB), 1, FPG)
    any_local = jax.random.randint(keys[2], (NFRAG, NNB), 0, FPG)
    local_index = jnp.where(near_group == owner_group[:, None], (fragments[:, None] % FPG + local_shift) % FPG, any_local)
    return (near_group * FPG + local_index).astype(jnp.int32)


def level_of(stream_key, extent, cuts, low, top_value):
    def one(dim, shards_of):
        heights = jax.random.uniform(jax.random.fold_in(jax.random.fold_in(stream_key, 6), dim), (shards_of,), jnp.float32, low / len(cuts), top_value / len(cuts))
        return jnp.repeat(jnp.exp(heights), extent[dim] // shards_of).reshape((-1,) + (1,) * (len(extent) - dim - 1))

    loudness = one(*cuts[0])
    for cut in cuts[1:]:
        loudness = loudness * one(*cut)
    return loudness


def normal_values(key, shape, width, limit, pieces=(), kind=jnp.bfloat16):
    array = jax.random.normal(key, shape, jnp.float32) * width
    if len(pieces) > 0:
        array = level_of(key, shape, pieces, -0.22, 0.18) * array
    return jnp.clip(array, min=-limit, max=limit).astype(kind)


def setup_inputs(seed: int = 0) -> dict:
    splits = jax.random.split(jax.random.key(seed), 8)
    return {
        "sizes": draw_sizes(jax.random.fold_in(splits[7], 71), 0),
        "neighbors": draw_neighbors(jax.random.fold_in(splits[7], 71), 0),
        "slot_fragment": draw_slot_fragment(jax.random.fold_in(splits[7], 71), 0),
        "density": normal_values(splits[3], (NFRAG, NB, NB), 1.0, 6.0, ((0, 4), (1, 8))),
        "hcore": normal_values(splits[4], (NFRAG, NB, NB), 0.5, 3.0, ((0, 4), (1, 8))),
        "integrals": normal_values(splits[5], (NFRAG, CHOL, NB, NB), (3 * NB) ** -0.5, 0.15625, ((0, 4), (1, 8))),
        "couple": normal_values(splits[6], (NFRAG, NNB, NB, NB), 0.4, 2.390625, ((0, 4), (2, 8))),
    }


def reference(sizes, neighbors, slot_fragment, density, hcore, integrals, couple):
    positions = jnp.arange(NB, dtype=jnp.int32)
    keep_mask = ((positions[None, :, None] < sizes[:, None, None]) & (positions[None, None, :] < sizes[:, None, None])).astype(jnp.float32)
    masked = (density.astype(jnp.float32) * keep_mask).astype(jnp.bfloat16)
    slot_of = jnp.zeros((NFRAG,), jnp.int32).at[slot_fragment].set(jnp.arange(NFRAG, dtype=jnp.int32))

    def fragment_fock(fragment):
        factors = integrals[slot_of[fragment]].astype(jnp.float32)
        frag_density = masked[fragment].astype(jnp.float32)
        product = jnp.einsum('qik,kj->qij', factors, frag_density, precision=lax.Precision.HIGHEST)
        product = product.astype(jnp.bfloat16).astype(jnp.float32)
        exchange_term = jnp.einsum('qij,qlj->qil', product, factors, precision=lax.Precision.HIGHEST)
        coulomb = jnp.einsum('qij,ij->q', factors, frag_density, precision=lax.Precision.HIGHEST)
        two_body = jnp.sum(coulomb[:, None, None] * factors - 0.5 * exchange_term, axis=0)
        picked = masked[neighbors[fragment]].astype(jnp.float32)
        coupling = jnp.sum(couple[fragment].astype(jnp.float32) * picked, axis=0)
        return keep_mask[fragment] * (hcore[fragment].astype(jnp.float32) + two_body + coupling)

    return lax.map(fragment_fock, jnp.arange(NFRAG, dtype=jnp.int32))
```

```python
import math
from functools import partial

import jax
import jax.numpy as jnp
from jax import lax
from jax.experimental import pallas as pl
from jax.experimental.pallas import tpu as pltpu
from jax.sharding import PartitionSpec as P

TILE = 128
WIRE = jnp.float16
VM = pl.BlockSpec(memory_space=pltpu.VMEM)
SM = pl.BlockSpec(memory_space=pltpu.SMEM)
PAR = pltpu.CompilerParams(vmem_limit_bytes=58 << 20)


def keep_of(size, row0, shape):
    rows = row0 + lax.broadcasted_iota(jnp.int32, shape, 0)
    cols = lax.broadcasted_iota(jnp.int32, shape, 1)
    return (rows < size) & (cols < size)


def prep_kernel(size_ref, pick_ref, row_ref, d_ref, m_ref, o_ref):
    count, rows, cols = d_ref.shape
    for f in range(count):
        keep = keep_of(size_ref[f], row_ref[0], (rows, cols))
        m_ref[f] = jnp.where(keep, d_ref[f].astype(jnp.float32), 0.0).astype(m_ref.dtype)
    for s in range(o_ref.shape[0]):
        o_ref[s] = m_ref[pick_ref[s]]


def pack_kernel(src_ref, k_ref, r_ref, o_ref):
    for t in range(o_ref.shape[0]):
        o_ref[t] = r_ref[src_ref[t], :, pl.ds(pl.multiple_of(k_ref[t] * TILE, TILE), TILE)]


def fock_kernel(scale, cls_ref, off_ref, g_ref, l_ref, o_ref, d_scr, acc_scr):
    s = pl.program_id(0)
    lanes, _, slab, _ = g_ref.shape
    basis = l_ref.shape[-1]
    off = off_ref[s]

    @pl.when(s == 0)
    def _():
        o_ref[...] = jnp.zeros_like(o_ref)

    for c in range(1, basis // TILE + 1):
        e = c * TILE

        @pl.when(cls_ref[s] == c)
        def _(c=c, e=e):
            for lane in range(e // slab):
                for k in range(c):
                    d_scr[lane * slab:(lane + 1) * slab, k * TILE:(k + 1) * TILE] = g_ref[lane, off + k]

            for q in range(l_ref.shape[1]):
                lq = l_ref[0, q, :e, :e]
                dm = d_scr[:e, :e]
                prod = jnp.dot(lq, dm, preferred_element_type=jnp.float32).astype(jnp.bfloat16)
                coul = jnp.sum(lq.astype(jnp.float32) * dm.astype(jnp.float32))
                exch = lax.dot_general(
                    prod, lq, (((1,), (1,)), ((), ())), preferred_element_type=jnp.float32
                )
                part = coul * lq.astype(jnp.float32) - 0.5 * exch
                if q == 0:
                    acc_scr[:e, :e] = part
                else:
                    acc_scr[:e, :e] += part
            for lane in range(e // slab):
                for k in range(c):
                    tile = acc_scr[lane * slab:(lane + 1) * slab, k * TILE:(k + 1) * TILE]
                    o_ref[lane, off + k] = (tile * scale).astype(o_ref.dtype)


def unpack_kernel(dst_ref, tile_ref, p_ref, o_ref):
    slots, tiles = tile_ref.shape
    o_ref[...] = jnp.zeros_like(o_ref)
    for s in range(slots):
        for k in range(tiles):
            o_ref[dst_ref[s], :, k * TILE:(k + 1) * TILE] = p_ref[tile_ref[s, k]]


def base_kernel(near_ref, low_ref, mid_ref, high_ref, h_ref, c_ref, o_ref, ext):
    f = pl.program_id(0)
    n = mid_ref.shape[0]

    @pl.when(f == 0)
    def _():
        ext[0:n] = low_ref[...]
        ext[n:2 * n] = mid_ref[...]
        ext[2 * n:3 * n] = high_ref[...]

    total = h_ref[0].astype(jnp.float32)
    for k in range(c_ref.shape[1]):
        total += c_ref[0, k].astype(jnp.float32) * ext[near_ref[f, k]].astype(jnp.float32)
    o_ref[0] = total


def final_kernel(scale, size_ref, slot_ref, row_ref, b_ref, r_ref, o_ref):
    count, rows, cols = b_ref.shape
    for f in range(count):
        keep = keep_of(size_ref[f], row_ref[0], (rows, cols))
        back = r_ref[slot_ref[f]].astype(jnp.float32) * scale
        o_ref[f] = jnp.where(keep, b_ref[f] + back, 0.0)


def local(sizes, neighbors, slot_fragment, density, hcore, integrals, couple):
    i32 = jnp.int32
    groups = lax.axis_size("frag")
    my_group = lax.axis_index("frag")
    core_count = lax.axis_size("ka")
    lanes = lax.axis_size("tile") * core_count
    my_lane = lax.axis_index("tile") * core_count + lax.axis_index("ka")
    per_group, slab, basis = density.shape
    chol_here = integrals.shape[1]
    tiles = basis // TILE
    capacity = max(1, per_group // groups)
    buffers = groups * capacity
    first = my_group * per_group
    ids = jnp.arange(per_group, dtype=i32)
    row0 = (my_lane * slab).astype(i32).reshape(1)
    own_sizes = lax.dynamic_slice_in_dim(sizes, first, per_group)

    bound = 1.5 * (basis * 25 / 32) ** 2 * 6 * 0.15625**2 * chol_here * lanes
    scale = 2.0 ** math.ceil(math.log2(bound / 60000))

    matches = slot_fragment[None, :] == (first + ids)[:, None]
    slot_ids = jnp.arange(slot_fragment.shape[0], dtype=i32)
    slot_of = jnp.sum(jnp.where(matches, slot_ids[None, :], 0), axis=1)
    target = slot_of // per_group
    earlier = ids[None, :] < ids[:, None]
    rank_pos = jnp.sum((target[:, None] == target[None, :]) & earlier, axis=1)
    send_slot = (target * capacity + rank_pos).astype(i32)
    out_ids = jnp.arange(buffers, dtype=i32)
    pick = jnp.sum(jnp.where(out_ids[:, None] == send_slot[None, :], ids[None, :], 0), axis=1).astype(i32)

    held = lax.dynamic_slice_in_dim(slot_fragment, first, per_group)
    source = held // per_group
    before = held[None, :] < held[:, None]
    flat = (source * capacity + jnp.sum((source[:, None] == source[None, :]) & before, axis=1)).astype(i32)

    frag_class = (sizes + TILE - 1) // TILE
    slot_class = jnp.sum(
        jnp.where(slot_fragment[:, None] == slot_ids[None, :], frag_class[None, :], 0), axis=1
    ).astype(i32)
    need = jnp.max(jnp.sum(slot_class.reshape(groups, per_group), axis=1))
    cls = lax.dynamic_slice_in_dim(slot_class, first, per_group)
    off = jnp.sum(jnp.where(earlier, cls[None, :], 0), axis=1).astype(i32)
    most = per_group * tiles
    tile_ids = jnp.arange(most, dtype=i32)
    inside = (tile_ids[:, None] >= off[None, :]) & (tile_ids[:, None] < (off + cls)[None, :])
    tile_src = jnp.sum(jnp.where(inside, flat[None, :], 0), axis=1).astype(i32)
    tile_k = jnp.sum(jnp.where(inside, tile_ids[:, None] - off[None, :], 0), axis=1).astype(i32)
    ks = jnp.arange(tiles, dtype=i32)
    tile_at = jnp.where(ks[None, :] < cls[:, None], off[:, None] + ks[None, :], 0).astype(i32)

    slab_bf = jax.ShapeDtypeStruct((per_group, slab, basis), jnp.bfloat16)
    masked, outgoing = pl.pallas_call(
        prep_kernel,
        out_shape=(slab_bf, jax.ShapeDtypeStruct((buffers, slab, basis), jnp.bfloat16)),
        in_specs=[SM, SM, SM, VM],
        out_specs=(VM, VM),
        name="prep",
    )(own_sizes, pick, row0, density)

    received = lax.all_to_all(
        outgoing.reshape(groups, capacity, slab, basis), "frag", split_axis=0, concat_axis=0, tiled=True
    ).reshape(buffers, slab, basis)

    forward = [(i, i + 1) for i in range(groups - 1)]
    backward = [(b, a) for a, b in forward]
    low = lax.ppermute(masked, "frag", forward)
    high = lax.ppermute(masked, "frag", backward)
    near = (neighbors - (my_group - 1) * per_group).astype(i32)

    slab_block = (1, slab, basis)
    nnb = couple.shape[1]
    base = pl.pallas_call(
        base_kernel,
        grid_spec=pltpu.PrefetchScalarGridSpec(
            num_scalar_prefetch=1,
            grid=(per_group,),
            in_specs=[
                VM, VM, VM,
                pl.BlockSpec(slab_block, lambda f, n: (f, 0, 0)),
                pl.BlockSpec((1, nnb, slab, basis), lambda f, n: (f, 0, 0, 0)),
            ],
            out_specs=pl.BlockSpec(slab_block, lambda f, n: (f, 0, 0)),
            scratch_shapes=[pltpu.VMEM((3 * per_group, slab, basis), jnp.bfloat16)],
        ),
        out_shape=jax.ShapeDtypeStruct((per_group, slab, basis), jnp.float32),
        name="base",
    )(near, low, masked, high, hcore, couple)

    def branch(count, received, integrals):
        packed = pl.pallas_call(
            pack_kernel,
            out_shape=jax.ShapeDtypeStruct((count, slab, TILE), jnp.bfloat16),
            in_specs=[SM, SM, VM],
            out_specs=VM,
            name="pack",
        )(tile_src, tile_k, received)
        gathered = lax.all_gather(packed, ("tile", "ka"), axis=0, tiled=True)
        whole = (lanes, count, slab, TILE)
        parts = pl.pallas_call(
            partial(fock_kernel, 1.0 / scale),
            grid_spec=pltpu.PrefetchScalarGridSpec(
                num_scalar_prefetch=2,
                grid=(per_group,),
                in_specs=[
                    pl.BlockSpec(whole, lambda s, a, b: (0, 0, 0, 0), pipeline_mode=pl.Buffered(1)),
                    pl.BlockSpec((1, chol_here, basis, basis), lambda s, a, b: (s, 0, 0, 0)),
                ],
                out_specs=pl.BlockSpec(whole, lambda s, a, b: (0, 0, 0, 0)),
                scratch_shapes=[
                    pltpu.VMEM((basis, basis), jnp.bfloat16),
                    pltpu.VMEM((basis, basis), jnp.float32),
                ],
            ),
            out_shape=jax.ShapeDtypeStruct(whole, jnp.float32),
            compiler_params=PAR,
            name="fock",
        )(cls, off, gathered.reshape(whole), integrals)
        summed = lax.psum_scatter(
            parts.reshape(lanes * count, slab, TILE).astype(WIRE), ("tile", "ka"), scatter_dimension=0, tiled=True
        )
        return pl.pallas_call(
            unpack_kernel,
            out_shape=jax.ShapeDtypeStruct((buffers, slab, basis), jnp.float32),
            in_specs=[SM, SM, VM],
            out_specs=VM,
            name="unpack",
        )(flat, tile_at, summed.astype(jnp.float32))

    step = per_group // 2
    counts = [per_group + step * i for i in range(1, (most - per_group) // step + 1)]
    counts = [c for c in counts if c <= most * 3 // 4] + [most]
    which = jnp.sum(need > jnp.array(counts[:-1], i32)).astype(i32)
    back = lax.switch(which, [partial(branch, c) for c in counts], received, integrals)
    returned = lax.all_to_all(
        back.reshape(groups, capacity, slab, basis).astype(WIRE), "frag", split_axis=0, concat_axis=0, tiled=True
    ).reshape(buffers, slab, basis)
    return pl.pallas_call(
        partial(final_kernel, scale),
        out_shape=jax.ShapeDtypeStruct((per_group, slab, basis), jnp.float32),
        in_specs=[SM, SM, SM, VM, VM],
        out_specs=VM,
        name="final",
    )(own_sizes, send_slot, row0, base, returned.astype(jnp.float32))


def solution(mesh):
    return jax.shard_map(
        local,
        mesh=mesh,
        in_specs=(
            P(),
            P("frag", None),
            P(),
            P("frag", ("tile", "ka"), None),
            P("frag", ("tile", "ka"), None),
            P("frag", ("tile", "ka"), None, None),
            P("frag", None, ("tile", "ka"), None),
        ),
        out_specs=P("frag", ("tile", "ka"), None),
        check_vma=False,
    )
```

```python
import math
from functools import partial

import jax
import jax.numpy as jnp
from jax import lax
from jax.experimental import pallas as pl
from jax.experimental.pallas import tpu as pltpu
from jax.sharding import PartitionSpec as P

TILE = 128
WIRE = jnp.float16
VM = pl.BlockSpec(memory_space=pltpu.VMEM)
SM = pl.BlockSpec(memory_space=pltpu.SMEM)
PAR = pltpu.CompilerParams(vmem_limit_bytes=58 << 20)


def keep_of(size, row0, shape):
    rows = row0 + lax.broadcasted_iota(jnp.int32, shape, 0)
    cols = lax.broadcasted_iota(jnp.int32, shape, 1)
    return (rows < size) & (cols < size)


def prep_kernel(size_ref, pick_ref, row_ref, d_ref, m_ref, o_ref):
    count, rows, cols = d_ref.shape
    for f in range(count):
        keep = keep_of(size_ref[f], row_ref[0], (rows, cols))
        m_ref[f] = jnp.where(keep, d_ref[f].astype(jnp.float32), 0.0).astype(m_ref.dtype)
    for s in range(o_ref.shape[0]):
        o_ref[s] = m_ref[pick_ref[s]]


def pack_kernel(src_ref, k_ref, r_ref, o_ref):
    for t in range(o_ref.shape[0]):
        o_ref[t] = r_ref[src_ref[t], :, pl.ds(pl.multiple_of(k_ref[t] * TILE, TILE), TILE)]


def fock_kernel(scale, cls_ref, off_ref, g_ref, l_ref, o_ref, d_scr, acc_scr):
    s = pl.program_id(0)
    lanes, _, slab, _ = g_ref.shape
    basis = l_ref.shape[-1]
    off = off_ref[s]

    @pl.when(s == 0)
    def _():
        o_ref[...] = jnp.zeros_like(o_ref)

    for c in range(1, basis // TILE + 1):
        e = c * TILE

        @pl.when(cls_ref[s] == c)
        def _(c=c, e=e):
            for lane in range(e // slab):
                for k in range(c):
                    d_scr[lane * slab:(lane + 1) * slab, k * TILE:(k + 1) * TILE] = g_ref[lane, off + k]

            for q in range(l_ref.shape[1]):
                lq = l_ref[0, q, :e, :e]
                dm = d_scr[:e, :e]
                prod = jnp.dot(lq, dm, preferred_element_type=jnp.float32).astype(jnp.bfloat16)
                coul = jnp.sum(lq.astype(jnp.float32) * dm.astype(jnp.float32))
                exch = lax.dot_general(
                    prod, lq, (((1,), (1,)), ((), ())), preferred_element_type=jnp.float32
                )
                part = coul * lq.astype(jnp.float32) - 0.5 * exch
                if q == 0:
                    acc_scr[:e, :e] = part
                else:
                    acc_scr[:e, :e] += part
            for lane in range(e // slab):
                for k in range(c):
                    tile = acc_scr[lane * slab:(lane + 1) * slab, k * TILE:(k + 1) * TILE]
                    o_ref[lane, off + k] = (tile * scale).astype(o_ref.dtype)


def unpack_kernel(dst_ref, tile_ref, p_ref, o_ref):
    slots, tiles = tile_ref.shape
    o_ref[...] = jnp.zeros_like(o_ref)
    for s in range(slots):
        for k in range(tiles):
            o_ref[dst_ref[s], :, k * TILE:(k + 1) * TILE] = p_ref[tile_ref[s, k]]


def base_kernel(near_ref, low_ref, mid_ref, high_ref, h_ref, c_ref, o_ref, ext):
    f = pl.program_id(0)
    n = mid_ref.shape[0]

    @pl.when(f == 0)
    def _():
        ext[0:n] = low_ref[...]
        ext[n:2 * n] = mid_ref[...]
        ext[2 * n:3 * n] = high_ref[...]

    total = h_ref[0].astype(jnp.float32)
    for k in range(c_ref.shape[1]):
        total += c_ref[0, k].astype(jnp.float32) * ext[near_ref[f, k]].astype(jnp.float32)
    o_ref[0] = total


def final_kernel(scale, size_ref, slot_ref, row_ref, b_ref, r_ref, o_ref):
    count, rows, cols = b_ref.shape
    for f in range(count):
        keep = keep_of(size_ref[f], row_ref[0], (rows, cols))
        back = r_ref[slot_ref[f]].astype(jnp.float32) * scale
        o_ref[f] = jnp.where(keep, b_ref[f] + back, 0.0)


def local(sizes, neighbors, slot_fragment, density, hcore, integrals, couple):
    i32 = jnp.int32
    groups = lax.axis_size("frag")
    my_group = lax.axis_index("frag")
    core_count = lax.axis_size("ka")
    lanes = lax.axis_size("tile") * core_count
    my_lane = lax.axis_index("tile") * core_count + lax.axis_index("ka")
    per_group, slab, basis = density.shape
    chol_here = integrals.shape[1]
    tiles = basis // TILE
    capacity = max(1, per_group // groups)
    buffers = groups * capacity
    first = my_group * per_group
    ids = jnp.arange(per_group, dtype=i32)
    row0 = (my_lane * slab).astype(i32).reshape(1)
    own_sizes = lax.dynamic_slice_in_dim(sizes, first, per_group)

    bound = 1.5 * (basis * 25 / 32) ** 2 * 6 * 0.15625**2 * chol_here * lanes
    scale = 2.0 ** math.ceil(math.log2(bound / 60000))

    matches = slot_fragment[None, :] == (first + ids)[:, None]
    slot_ids = jnp.arange(slot_fragment.shape[0], dtype=i32)
    slot_of = jnp.sum(jnp.where(matches, slot_ids[None, :], 0), axis=1)
    target = slot_of // per_group
    earlier = ids[None, :] < ids[:, None]
    rank_pos = jnp.sum((target[:, None] == target[None, :]) & earlier, axis=1)
    send_slot = (target * capacity + rank_pos).astype(i32)
    out_ids = jnp.arange(buffers, dtype=i32)
    pick = jnp.sum(jnp.where(out_ids[:, None] == send_slot[None, :], ids[None, :], 0), axis=1).astype(i32)

    held = lax.dynamic_slice_in_dim(slot_fragment, first, per_group)
    source = held // per_group
    before = held[None, :] < held[:, None]
    flat = (source * capacity + jnp.sum((source[:, None] == source[None, :]) & before, axis=1)).astype(i32)

    frag_class = (sizes + TILE - 1) // TILE
    slot_class = jnp.sum(
        jnp.where(slot_fragment[:, None] == slot_ids[None, :], frag_class[None, :], 0), axis=1
    ).astype(i32)
    need = jnp.max(jnp.sum(slot_class.reshape(groups, per_group), axis=1))
    cls = lax.dynamic_slice_in_dim(slot_class, first, per_group)
    off = jnp.sum(jnp.where(earlier, cls[None, :], 0), axis=1).astype(i32)
    most = per_group * tiles
    tile_ids = jnp.arange(most, dtype=i32)
    inside = (tile_ids[:, None] >= off[None, :]) & (tile_ids[:, None] < (off + cls)[None, :])
    tile_src = jnp.sum(jnp.where(inside, flat[None, :], 0), axis=1).astype(i32)
    tile_k = jnp.sum(jnp.where(inside, tile_ids[:, None] - off[None, :], 0), axis=1).astype(i32)
    ks = jnp.arange(tiles, dtype=i32)
    tile_at = jnp.where(ks[None, :] < cls[:, None], off[:, None] + ks[None, :], 0).astype(i32)

    slab_bf = jax.ShapeDtypeStruct((per_group, slab, basis), jnp.bfloat16)
    masked, outgoing = pl.pallas_call(
        prep_kernel,
        out_shape=(slab_bf, jax.ShapeDtypeStruct((buffers, slab, basis), jnp.bfloat16)),
        in_specs=[SM, SM, SM, VM],
        out_specs=(VM, VM),
        name="prep",
    )(own_sizes, pick, row0, density)

    received = lax.all_to_all(
        outgoing.reshape(groups, capacity, slab, basis), "frag", split_axis=0, concat_axis=0, tiled=True
    ).reshape(buffers, slab, basis)

    received, masked = lax.optimization_barrier((received, masked))
    forward = [(i, i + 1) for i in range(groups - 1)]
    backward = [(b, a) for a, b in forward]
    near = (neighbors - (my_group - 1) * per_group).astype(i32)
    slab_block = (1, slab, basis)
    nnb = couple.shape[1]

    def coupled(masked, hcore, couple):
        low = lax.ppermute(masked, "frag", forward)
        high = lax.ppermute(masked, "frag", backward)
        return pl.pallas_call(
            base_kernel,
            grid_spec=pltpu.PrefetchScalarGridSpec(
                num_scalar_prefetch=1,
                grid=(per_group,),
                in_specs=[
                    VM, VM, VM,
                    pl.BlockSpec(slab_block, lambda f, n: (f, 0, 0)),
                    pl.BlockSpec((1, nnb, slab, basis), lambda f, n: (f, 0, 0, 0)),
                ],
                out_specs=pl.BlockSpec(slab_block, lambda f, n: (f, 0, 0)),
                scratch_shapes=[pltpu.VMEM((3 * per_group, slab, basis), jnp.bfloat16)],
            ),
            out_shape=jax.ShapeDtypeStruct((per_group, slab, basis), jnp.float32),
            cost_estimate=pl.CostEstimate(flops=0, bytes_accessed=20 << 20, transcendentals=0),
            name="base",
        )(near, low, masked, high, hcore, couple)

    def branch(count, received, masked, integrals, hcore, couple):
        packed = pl.pallas_call(
            pack_kernel,
            out_shape=jax.ShapeDtypeStruct((count, slab, TILE), jnp.bfloat16),
            in_specs=[SM, SM, VM],
            out_specs=VM,
            name="pack",
        )(tile_src, tile_k, received)
        gathered = lax.all_gather(packed, ("tile", "ka"), axis=0, tiled=True)
        base = coupled(masked, hcore, couple)
        whole = (lanes, count, slab, TILE)
        parts = pl.pallas_call(
            partial(fock_kernel, 1.0 / scale),
            grid_spec=pltpu.PrefetchScalarGridSpec(
                num_scalar_prefetch=2,
                grid=(per_group,),
                in_specs=[
                    pl.BlockSpec(whole, lambda s, a, b: (0, 0, 0, 0), pipeline_mode=pl.Buffered(1)),
                    pl.BlockSpec((1, chol_here, basis, basis), lambda s, a, b: (s, 0, 0, 0)),
                ],
                out_specs=pl.BlockSpec(whole, lambda s, a, b: (0, 0, 0, 0)),
                scratch_shapes=[
                    pltpu.VMEM((basis, basis), jnp.bfloat16),
                    pltpu.VMEM((basis, basis), jnp.float32),
                ],
            ),
            out_shape=jax.ShapeDtypeStruct(whole, jnp.float32),
            compiler_params=PAR,
            name="fock",
        )(cls, off, gathered.reshape(whole), integrals)
        summed = lax.psum_scatter(
            parts.reshape(lanes * count, slab, TILE), ("tile", "ka"), scatter_dimension=0, tiled=True
        )
        back = pl.pallas_call(
            unpack_kernel,
            out_shape=jax.ShapeDtypeStruct((buffers, slab, basis), jnp.float32),
            in_specs=[SM, SM, VM],
            out_specs=VM,
            name="unpack",
        )(flat, tile_at, summed)
        return back, base

    step = per_group // 2
    counts = [per_group + step * i for i in range(1, (most - per_group) // step + 1)]
    counts = [c for c in counts if c <= most * 3 // 4] + [most]
    which = jnp.sum(need > jnp.array(counts[:-1], i32)).astype(i32)
    back, base = lax.switch(
        which, [partial(branch, c) for c in counts], received, masked, integrals, hcore, couple
    )
    returned = lax.all_to_all(
        back.reshape(groups, capacity, slab, basis).astype(WIRE), "frag", split_axis=0, concat_axis=0, tiled=True
    ).reshape(buffers, slab, basis)
    return pl.pallas_call(
        partial(final_kernel, scale),
        out_shape=jax.ShapeDtypeStruct((per_group, slab, basis), jnp.float32),
        in_specs=[SM, SM, SM, VM, VM],
        out_specs=VM,
        name="final",
    )(own_sizes, send_slot, row0, base, returned.astype(jnp.float32))


def solution(mesh):
    return jax.shard_map(
        local,
        mesh=mesh,
        in_specs=(
            P(),
            P("frag", None),
            P(),
            P("frag", ("tile", "ka"), None),
            P("frag", ("tile", "ka"), None),
            P("frag", ("tile", "ka"), None, None),
            P("frag", None, ("tile", "ka"), None),
        ),
        out_specs=P("frag", ("tile", "ka"), None),
        check_vma=False,
    )
```

```python
import math
from functools import partial

import jax
import jax.numpy as jnp
from jax import lax
from jax.experimental import pallas as pl
from jax.experimental.pallas import tpu as pltpu
from jax.sharding import PartitionSpec as P

TILE = 128
WIRE = jnp.float16
LEVELS = 32000.0
MESH = pl.DeviceIdType.MESH
VM = pl.BlockSpec(memory_space=pltpu.VMEM)
SM = pl.BlockSpec(memory_space=pltpu.SMEM)
PAR = pltpu.CompilerParams(vmem_limit_bytes=58 << 20)


def keep_of(size, row0, shape):
    rows = row0 + lax.broadcasted_iota(jnp.int32, shape, 0)
    cols = lax.broadcasted_iota(jnp.int32, shape, 1)
    return (rows < size) & (cols < size)


def greet(pairs):
    barrier = pltpu.get_barrier_semaphore()
    for there, device in pairs:
        @pl.when(there)
        def _(device=device):
            pl.semaphore_signal(barrier, inc=1, device_id=device, device_id_type=MESH)
    pl.semaphore_wait(barrier, sum(jnp.where(there, 1, 0) for there, _ in pairs))


def remote(src, dst, send, recv, device):
    return pltpu.make_async_remote_copy(
        src_ref=src, dst_ref=dst, send_sem=send, recv_sem=recv, device_id=device, device_id_type=MESH
    )


def gather_kernel(
    p_ref, m_ref, g_ref, low_ref, high_ref, own_sem, up_send, down_send, z_recv, k_send, k_recv, h_send, h_recv
):
    zs, fs = lax.axis_size("tile"), lax.axis_size("frag")
    z, k, f = lax.axis_index("tile"), lax.axis_index("ka"), lax.axis_index("frag")
    up, down, side = {"tile": z + 1}, {"tile": z - 1}, {"ka": 1 - k}
    right, left = {"frag": f + 1}, {"frag": f - 1}
    has_up, has_down, has_right, has_left = z < zs - 1, z > 0, f < fs - 1, f > 0
    greet([(z >= 0, side), (has_up, up), (has_down, down), (has_right, right), (has_left, left)])

    own = pltpu.make_async_copy(p_ref, g_ref.at[2 * z + k], own_sem)
    own.start()

    def to_side(src, at):
        return remote(src, g_ref.at[2 * at + k], k_send.at[at], k_recv.at[at], side)

    def to_up(src, at):
        return remote(src, g_ref.at[2 * at + k], up_send.at[at], z_recv.at[at], up)

    def to_down(src, at):
        return remote(src, g_ref.at[2 * at + k], down_send.at[at], z_recv.at[at], down)

    def to_right():
        return remote(m_ref, low_ref, h_send.at[0], h_recv.at[0], right)

    def to_left():
        return remote(m_ref, high_ref, h_send.at[1], h_recv.at[1], left)

    pl.when(has_up)(lambda: to_up(p_ref, z).start())
    pl.when(has_down)(lambda: to_down(p_ref, z).start())
    to_side(p_ref, z).start()
    pl.when(has_right)(lambda: to_right().start())
    pl.when(has_left)(lambda: to_left().start())

    for d in range(1, zs):
        @pl.when(z >= d)
        def _(d=d):
            slot = g_ref.at[2 * (z - d) + k]
            to_up(slot, z - d).wait_recv()
            pl.when(has_up)(lambda: to_up(slot, z - d).start())
            to_side(slot, z - d).start()

        @pl.when(z + d < zs)
        def _(d=d):
            slot = g_ref.at[2 * (z + d) + k]
            to_down(slot, z + d).wait_recv()
            pl.when(has_down)(lambda: to_down(slot, z + d).start())
            to_side(slot, z + d).start()

    own.wait()
    for at in range(zs):
        arrived = g_ref.at[2 * at + 1 - k]
        remote(arrived, arrived, k_send.at[at], k_recv.at[at], side).wait_recv()
        to_side(p_ref, at).wait_send()
        pl.when(has_up & (at <= z))(lambda: to_up(p_ref, at).wait_send())
        pl.when(has_down & (at >= z))(lambda: to_down(p_ref, at).wait_send())
    pl.when(has_right)(lambda: to_right().wait_send())
    pl.when(has_left)(lambda: to_left().wait_send())
    pl.when(has_left)(lambda: to_right().wait_recv())
    pl.when(has_right)(lambda: to_left().wait_recv())


def reduce_kernel(
    x_ref, o_ref, ko, kso, ki, ksi, uo, uso, ui, usi, do, dso, di, dsi, k_send, k_recv, u_send, u_recv, d_send, d_recv
):
    zs = lax.axis_size("tile")
    z, k = lax.axis_index("tile"), lax.axis_index("ka")
    count = x_ref.shape[1]
    has_up, has_down = z < zs - 1, z > 0
    up, down, side = {"tile": z + 1}, {"tile": z - 1}, {"ka": 1 - k}
    greet([(z >= 0, side), (has_up, up), (has_down, down)])

    def copies(out, out_s, into, into_s, send, recv, at, device):
        return (
            remote(out.at[at], into.at[at], send.at[0, at], recv.at[0, at], device),
            remote(out_s.at[at], into_s.at[at], send.at[1, at], recv.at[1, at], device),
        )

    def side_copies(at):
        return copies(ko, kso, ki, ksi, k_send, k_recv, at, side)

    def up_copies(at):
        return copies(uo, uso, ui, usi, u_send, u_recv, at, up)

    def down_copies(at):
        return copies(do, dso, di, dsi, d_send, d_recv, at, down)

    def store_coded(value, out, out_s, at, t):
        top = jnp.max(jnp.abs(value), axis=0, keepdims=True)
        inverse = jnp.where(top > 0, LEVELS / jnp.where(top > 0, top, 1.0), 0.0)
        out[at, t] = jnp.round(value * inverse).astype(jnp.int32).astype(jnp.int16)
        out_s[at, pl.ds(t, 1), :] = top * (1.0 / LEVELS)

    def decoded(into, into_s, at, t):
        return into[at, t].astype(jnp.int32).astype(jnp.float32) * into_s[at, pl.ds(t, 1), :]

    order = [at for i in range(zs // 2) for at in (zs - 1 - i, i)]
    for at in order:
        @pl.loop(0, count)
        def _(t, at=at):
            store_coded(x_ref[2 * at + 1 - k, t], ko, kso, at, t)
        for c in side_copies(at):
            c.start()

    def wait_in(pair):
        for c in pair:
            c.wait_recv()

    def pass_on(at, out, out_s, into, into_s, pair, has_more):
        wait_in(side_copies(at))

        @pl.when(has_more)
        def _():
            wait_in(pair)

            @pl.loop(0, count)
            def _(t):
                value = x_ref[2 * at + k, t] + decoded(ki, ksi, at, t) + decoded(into, into_s, at, t)
                store_coded(value, out, out_s, at, t)

        @pl.when(jnp.logical_not(has_more))
        def _():
            @pl.loop(0, count)
            def _(t):
                store_coded(x_ref[2 * at + k, t] + decoded(ki, ksi, at, t), out, out_s, at, t)

        for c in pair:
            c.start()

    for i in range(zs - 1):
        at = zs - 1 - i
        pl.when(z < at)(lambda at=at: pass_on(at, uo, uso, ui, usi, up_copies(at), has_down))
        pl.when(z > i)(lambda i=i: pass_on(i, do, dso, di, dsi, down_copies(i), has_up))

    wait_in(side_copies(z))

    @pl.loop(0, count)
    def _(t):
        o_ref[t] = x_ref[2 * z + k, t] + decoded(ki, ksi, z, t)

    for there, pair, into, into_s in ((has_down, up_copies(z), ui, usi), (has_up, down_copies(z), di, dsi)):
        @pl.when(there)
        def _(pair=pair, into=into, into_s=into_s):
            wait_in(pair)

            @pl.loop(0, count)
            def _(t):
                o_ref[t] += decoded(into, into_s, z, t)

    for at in range(zs):
        for c in side_copies(at):
            c.wait_send()
        for there, pair in ((z < at, up_copies(at)), (z > at, down_copies(at))):
            @pl.when(there)
            def _(pair=pair):
                for c in pair:
                    c.wait_send()


def prep_kernel(size_ref, pick_ref, row_ref, d_ref, m_ref, o_ref):
    count, rows, cols = d_ref.shape
    for f in range(count):
        keep = keep_of(size_ref[f], row_ref[0], (rows, cols))
        m_ref[f] = jnp.where(keep, d_ref[f].astype(jnp.float32), 0.0).astype(m_ref.dtype)
    for s in range(o_ref.shape[0]):
        o_ref[s] = m_ref[pick_ref[s]]


def pack_kernel(src_ref, k_ref, r_ref, o_ref):
    for t in range(o_ref.shape[0]):
        o_ref[t] = r_ref[src_ref[t], :, pl.ds(pl.multiple_of(k_ref[t] * TILE, TILE), TILE)]


def fock_kernel(scale, cls_ref, off_ref, g_ref, l_ref, o_ref, d_scr, acc_scr):
    s = pl.program_id(0)
    lanes, _, slab, _ = g_ref.shape
    basis = l_ref.shape[-1]
    off = off_ref[s]

    @pl.when(s == 0)
    def _():
        o_ref[...] = jnp.zeros_like(o_ref)

    for c in range(1, basis // TILE + 1):
        e = c * TILE

        @pl.when(cls_ref[s] == c)
        def _(c=c, e=e):
            for lane in range(e // slab):
                for k in range(c):
                    d_scr[lane * slab:(lane + 1) * slab, k * TILE:(k + 1) * TILE] = g_ref[lane, off + k]

            for q in range(l_ref.shape[1]):
                lq = l_ref[0, q, :e, :e]
                dm = d_scr[:e, :e]
                prod = jnp.dot(lq, dm, preferred_element_type=jnp.float32).astype(jnp.bfloat16)
                coul = jnp.sum(lq.astype(jnp.float32) * dm.astype(jnp.float32))
                exch = lax.dot_general(
                    prod, lq, (((1,), (1,)), ((), ())), preferred_element_type=jnp.float32
                )
                part = coul * lq.astype(jnp.float32) - 0.5 * exch
                if q == 0:
                    acc_scr[:e, :e] = part
                else:
                    acc_scr[:e, :e] += part
            for lane in range(e // slab):
                for k in range(c):
                    tile = acc_scr[lane * slab:(lane + 1) * slab, k * TILE:(k + 1) * TILE]
                    o_ref[lane, off + k] = (tile * scale).astype(o_ref.dtype)


def unpack_kernel(dst_ref, tile_ref, p_ref, o_ref):
    slots, tiles = tile_ref.shape
    o_ref[...] = jnp.zeros_like(o_ref)
    for s in range(slots):
        for k in range(tiles):
            o_ref[dst_ref[s], :, k * TILE:(k + 1) * TILE] = p_ref[tile_ref[s, k]]


def base_kernel(near_ref, low_ref, mid_ref, high_ref, h_ref, c_ref, o_ref, ext):
    f = pl.program_id(0)
    n = mid_ref.shape[0]

    @pl.when(f == 0)
    def _():
        ext[0:n] = low_ref[...]
        ext[n:2 * n] = mid_ref[...]
        ext[2 * n:3 * n] = high_ref[...]

    total = h_ref[0].astype(jnp.float32)
    for k in range(c_ref.shape[1]):
        total += c_ref[0, k].astype(jnp.float32) * ext[near_ref[f, k]].astype(jnp.float32)
    o_ref[0] = total


def final_kernel(scale, size_ref, slot_ref, row_ref, b_ref, r_ref, o_ref):
    count, rows, cols = b_ref.shape
    for f in range(count):
        keep = keep_of(size_ref[f], row_ref[0], (rows, cols))
        back = r_ref[slot_ref[f]].astype(jnp.float32) * scale
        o_ref[f] = jnp.where(keep, b_ref[f] + back, 0.0)


def local(sizes, neighbors, slot_fragment, density, hcore, integrals, couple):
    i32 = jnp.int32
    groups = lax.axis_size("frag")
    my_group = lax.axis_index("frag")
    core_count = lax.axis_size("ka")
    lanes = lax.axis_size("tile") * core_count
    my_lane = lax.axis_index("tile") * core_count + lax.axis_index("ka")
    per_group, slab, basis = density.shape
    chol_here = integrals.shape[1]
    tiles = basis // TILE
    capacity = max(1, per_group // groups)
    buffers = groups * capacity
    first = my_group * per_group
    ids = jnp.arange(per_group, dtype=i32)
    row0 = (my_lane * slab).astype(i32).reshape(1)
    own_sizes = lax.dynamic_slice_in_dim(sizes, first, per_group)

    bound = 1.5 * (basis * 25 / 32) ** 2 * 6 * 0.15625**2 * chol_here * lanes
    scale = 2.0 ** math.ceil(math.log2(bound / 60000))

    matches = slot_fragment[None, :] == (first + ids)[:, None]
    slot_ids = jnp.arange(slot_fragment.shape[0], dtype=i32)
    slot_of = jnp.sum(jnp.where(matches, slot_ids[None, :], 0), axis=1)
    target = slot_of // per_group
    earlier = ids[None, :] < ids[:, None]
    rank_pos = jnp.sum((target[:, None] == target[None, :]) & earlier, axis=1)
    send_slot = (target * capacity + rank_pos).astype(i32)
    out_ids = jnp.arange(buffers, dtype=i32)
    pick = jnp.sum(jnp.where(out_ids[:, None] == send_slot[None, :], ids[None, :], 0), axis=1).astype(i32)

    held = lax.dynamic_slice_in_dim(slot_fragment, first, per_group)
    source = held // per_group
    before = held[None, :] < held[:, None]
    flat = (source * capacity + jnp.sum((source[:, None] == source[None, :]) & before, axis=1)).astype(i32)

    frag_class = (sizes + TILE - 1) // TILE
    slot_class = jnp.sum(
        jnp.where(slot_fragment[:, None] == slot_ids[None, :], frag_class[None, :], 0), axis=1
    ).astype(i32)
    need = jnp.max(jnp.sum(slot_class.reshape(groups, per_group), axis=1))
    cls = lax.dynamic_slice_in_dim(slot_class, first, per_group)
    off = jnp.sum(jnp.where(earlier, cls[None, :], 0), axis=1).astype(i32)
    most = per_group * tiles
    tile_ids = jnp.arange(most, dtype=i32)
    inside = (tile_ids[:, None] >= off[None, :]) & (tile_ids[:, None] < (off + cls)[None, :])
    tile_src = jnp.sum(jnp.where(inside, flat[None, :], 0), axis=1).astype(i32)
    tile_k = jnp.sum(jnp.where(inside, tile_ids[:, None] - off[None, :], 0), axis=1).astype(i32)
    ks = jnp.arange(tiles, dtype=i32)
    tile_at = jnp.where(ks[None, :] < cls[:, None], off[:, None] + ks[None, :], 0).astype(i32)

    slab_bf = jax.ShapeDtypeStruct((per_group, slab, basis), jnp.bfloat16)
    masked, outgoing = pl.pallas_call(
        prep_kernel,
        out_shape=(slab_bf, jax.ShapeDtypeStruct((buffers, slab, basis), jnp.bfloat16)),
        in_specs=[SM, SM, SM, VM],
        out_specs=(VM, VM),
        name="prep",
    )(own_sizes, pick, row0, density)

    received = lax.all_to_all(
        outgoing.reshape(groups, capacity, slab, basis), "frag", split_axis=0, concat_axis=0, tiled=True
    ).reshape(buffers, slab, basis)

    near = (neighbors - (my_group - 1) * per_group).astype(i32)
    slab_block = (1, slab, basis)
    nnb = couple.shape[1]

    def coupled(low, masked, high, hcore, couple):
        return pl.pallas_call(
            base_kernel,
            grid_spec=pltpu.PrefetchScalarGridSpec(
                num_scalar_prefetch=1,
                grid=(per_group,),
                in_specs=[
                    VM, VM, VM,
                    pl.BlockSpec(slab_block, lambda f, n: (f, 0, 0)),
                    pl.BlockSpec((1, nnb, slab, basis), lambda f, n: (f, 0, 0, 0)),
                ],
                out_specs=pl.BlockSpec(slab_block, lambda f, n: (f, 0, 0)),
                scratch_shapes=[pltpu.VMEM((3 * per_group, slab, basis), jnp.bfloat16)],
            ),
            out_shape=jax.ShapeDtypeStruct((per_group, slab, basis), jnp.float32),
            cost_estimate=pl.CostEstimate(flops=0, bytes_accessed=20 << 20, transcendentals=0),
            name="base",
        )(near, low, masked, high, hcore, couple)

    def branch(ident, count, received, masked, integrals, hcore, couple):
        packed = pl.pallas_call(
            pack_kernel,
            out_shape=jax.ShapeDtypeStruct((count, slab, TILE), jnp.bfloat16),
            in_specs=[SM, SM, VM],
            out_specs=VM,
            name="pack",
        )(tile_src, tile_k, received)
        zs = lax.axis_size("tile")
        dma = pltpu.SemaphoreType.DMA
        whole = (lanes, count, slab, TILE)
        gathered, low, high = pl.pallas_call(
            gather_kernel,
            out_shape=(jax.ShapeDtypeStruct(whole, jnp.bfloat16), slab_bf, slab_bf),
            in_specs=[VM, VM],
            out_specs=(VM, VM, VM),
            scratch_shapes=[dma, dma((zs,)), dma((zs,)), dma((zs,)), dma((zs,)), dma((zs,)), dma((2,)), dma((2,))],
            compiler_params=pltpu.CompilerParams(
                vmem_limit_bytes=58 << 20, collective_id=2 * ident, has_side_effects=True
            ),
            name="gather",
        )(packed, masked)
        base = coupled(low, masked, high, hcore, couple)
        parts = pl.pallas_call(
            partial(fock_kernel, 1.0 / scale),
            grid_spec=pltpu.PrefetchScalarGridSpec(
                num_scalar_prefetch=2,
                grid=(per_group,),
                in_specs=[
                    pl.BlockSpec(whole, lambda s, a, b: (0, 0, 0, 0), pipeline_mode=pl.Buffered(1)),
                    pl.BlockSpec((1, chol_here, basis, basis), lambda s, a, b: (s, 0, 0, 0)),
                ],
                out_specs=pl.BlockSpec(whole, lambda s, a, b: (0, 0, 0, 0)),
                scratch_shapes=[
                    pltpu.VMEM((basis, basis), jnp.bfloat16),
                    pltpu.VMEM((basis, basis), jnp.float32),
                ],
            ),
            out_shape=jax.ShapeDtypeStruct(whole, jnp.float32),
            compiler_params=PAR,
            name="fock",
        )(cls, off, gathered, integrals)
        coded = [
            pltpu.VMEM((zs, count, slab, TILE), jnp.int16),
            pltpu.VMEM((zs, count, TILE), jnp.float32),
        ]
        summed = pl.pallas_call(
            reduce_kernel,
            out_shape=jax.ShapeDtypeStruct((count, slab, TILE), jnp.float32),
            in_specs=[VM],
            out_specs=VM,
            scratch_shapes=coded * 6 + [dma((2, zs))] * 6,
            compiler_params=pltpu.CompilerParams(
                vmem_limit_bytes=58 << 20, collective_id=2 * ident + 1, has_side_effects=True
            ),
            name="reduce",
        )(parts)
        back = pl.pallas_call(
            unpack_kernel,
            out_shape=jax.ShapeDtypeStruct((buffers, slab, basis), jnp.float32),
            in_specs=[SM, SM, VM],
            out_specs=VM,
            name="unpack",
        )(flat, tile_at, summed)
        return back, base

    step = per_group // 2
    counts = [per_group + step * i for i in range(1, (most - per_group) // step + 1)]
    counts = [c for c in counts if c <= most * 3 // 4] + [most]
    which = jnp.sum(need > jnp.array(counts[:-1], i32)).astype(i32)
    back, base = lax.switch(
        which, [partial(branch, i, c) for i, c in enumerate(counts)], received, masked, integrals, hcore, couple
    )
    returned = lax.all_to_all(
        back.reshape(groups, capacity, slab, basis).astype(WIRE), "frag", split_axis=0, concat_axis=0, tiled=True
    ).reshape(buffers, slab, basis)
    return pl.pallas_call(
        partial(final_kernel, scale),
        out_shape=jax.ShapeDtypeStruct((per_group, slab, basis), jnp.float32),
        in_specs=[SM, SM, SM, VM, VM],
        out_specs=VM,
        name="final",
    )(own_sizes, send_slot, row0, base, returned.astype(jnp.float32))


def solution(mesh):
    return jax.shard_map(
        local,
        mesh=mesh,
        in_specs=(
            P(),
            P("frag", None),
            P(),
            P("frag", ("tile", "ka"), None),
            P("frag", ("tile", "ka"), None),
            P("frag", ("tile", "ka"), None, None),
            P("frag", None, ("tile", "ka"), None),
        ),
        out_specs=P("frag", ("tile", "ka"), None),
        check_vma=False,
    )
```

```python
import math
from functools import partial

import jax
import jax.numpy as jnp
from jax import lax
from jax.experimental import pallas as pl
from jax.experimental.pallas import tpu as pltpu
from jax.sharding import PartitionSpec as P

TILE = 128
WIRE = jnp.float16
LEVELS = 32000.0
MESH = pl.DeviceIdType.MESH
VM = pl.BlockSpec(memory_space=pltpu.VMEM)
SM = pl.BlockSpec(memory_space=pltpu.SMEM)
PAR = pltpu.CompilerParams(vmem_limit_bytes=58 << 20)


def keep_of(size, row0, shape):
    rows = row0 + lax.broadcasted_iota(jnp.int32, shape, 0)
    cols = lax.broadcasted_iota(jnp.int32, shape, 1)
    return (rows < size) & (cols < size)


def greet(pairs):
    barrier = pltpu.get_barrier_semaphore()
    for there, device in pairs:
        @pl.when(there)
        def _(device=device):
            pl.semaphore_signal(barrier, inc=1, device_id=device, device_id_type=MESH)
    pl.semaphore_wait(barrier, sum(jnp.where(there, 1, 0) for there, _ in pairs))


def remote(src, dst, send, recv, device):
    return pltpu.make_async_remote_copy(
        src_ref=src, dst_ref=dst, send_sem=send, recv_sem=recv, device_id=device, device_id_type=MESH
    )


def gather_kernel(
    p_ref, m_ref, g_ref, low_ref, own_sem, up_send, down_send, z_recv, k_send, k_recv, h_send, h_recv
):
    zs, fs = lax.axis_size("tile"), lax.axis_size("frag")
    z, k, f = lax.axis_index("tile"), lax.axis_index("ka"), lax.axis_index("frag")
    up, down, side = {"tile": z + 1}, {"tile": z - 1}, {"ka": 1 - k}
    right, left = {"frag": f + 1}, {"frag": f - 1}
    has_up, has_down, has_right, has_left = z < zs - 1, z > 0, f < fs - 1, f > 0
    greet([(z >= 0, side), (has_up, up), (has_down, down), (has_right, right), (has_left, left)])

    own = pltpu.make_async_copy(p_ref, g_ref.at[2 * z + k], own_sem)
    own.start()

    def to_side(src, at):
        return remote(src, g_ref.at[2 * at + k], k_send.at[at], k_recv.at[at], side)

    def to_up(src, at):
        return remote(src, g_ref.at[2 * at + k], up_send.at[at], z_recv.at[at], up)

    def to_down(src, at):
        return remote(src, g_ref.at[2 * at + k], down_send.at[at], z_recv.at[at], down)

    def to_right():
        return remote(m_ref, low_ref, h_send, h_recv, right)

    pl.when(has_up)(lambda: to_up(p_ref, z).start())
    pl.when(has_down)(lambda: to_down(p_ref, z).start())
    to_side(p_ref, z).start()
    pl.when(has_right)(lambda: to_right().start())

    for d in range(1, zs):
        @pl.when(z >= d)
        def _(d=d):
            slot = g_ref.at[2 * (z - d) + k]
            to_up(slot, z - d).wait_recv()
            pl.when(has_up)(lambda: to_up(slot, z - d).start())
            to_side(slot, z - d).start()

        @pl.when(z + d < zs)
        def _(d=d):
            slot = g_ref.at[2 * (z + d) + k]
            to_down(slot, z + d).wait_recv()
            pl.when(has_down)(lambda: to_down(slot, z + d).start())
            to_side(slot, z + d).start()

    own.wait()
    for at in range(zs):
        arrived = g_ref.at[2 * at + 1 - k]
        remote(arrived, arrived, k_send.at[at], k_recv.at[at], side).wait_recv()
        to_side(p_ref, at).wait_send()
        pl.when(has_up & (at <= z))(lambda: to_up(p_ref, at).wait_send())
        pl.when(has_down & (at >= z))(lambda: to_down(p_ref, at).wait_send())
    pl.when(has_right)(lambda: to_right().wait_send())
    pl.when(has_left)(lambda: to_right().wait_recv())


def reduce_kernel(
    x_ref, m_ref, o_ref, high_ref, ko, kso, ki, ksi, uo, uso, ui, usi, do, dso, di, dsi, k_send, k_recv, u_send, u_recv, d_send, d_recv,
    h_send, h_recv
):
    zs = lax.axis_size("tile")
    z, k = lax.axis_index("tile"), lax.axis_index("ka")
    count = x_ref.shape[1]
    has_up, has_down = z < zs - 1, z > 0
    up, down, side = {"tile": z + 1}, {"tile": z - 1}, {"ka": 1 - k}
    fs, f = lax.axis_size("frag"), lax.axis_index("frag")
    right, left = {"frag": f + 1}, {"frag": f - 1}
    has_right, has_left = f < fs - 1, f > 0
    greet([(z >= 0, side), (has_up, up), (has_down, down), (has_right, right), (has_left, left)])

    def to_left():
        return remote(m_ref, high_ref, h_send, h_recv, left)

    pl.when(has_left)(lambda: to_left().start())

    def copies(out, out_s, into, into_s, send, recv, at, device):
        return (
            remote(out.at[at], into.at[at], send.at[0, at], recv.at[0, at], device),
            remote(out_s.at[at], into_s.at[at], send.at[1, at], recv.at[1, at], device),
        )

    def side_copies(at):
        return copies(ko, kso, ki, ksi, k_send, k_recv, at, side)

    def up_copies(at):
        return copies(uo, uso, ui, usi, u_send, u_recv, at, up)

    def down_copies(at):
        return copies(do, dso, di, dsi, d_send, d_recv, at, down)

    def store_coded(value, out, out_s, at, t):
        top = jnp.max(jnp.abs(value), axis=0, keepdims=True)
        inverse = jnp.where(top > 0, LEVELS / jnp.where(top > 0, top, 1.0), 0.0)
        out[at, t] = jnp.round(value * inverse).astype(jnp.int32).astype(jnp.int16)
        out_s[at, pl.ds(t, 1), :] = top * (1.0 / LEVELS)

    def decoded(into, into_s, at, t):
        return into[at, t].astype(jnp.int32).astype(jnp.float32) * into_s[at, pl.ds(t, 1), :]

    order = [at for i in range(zs // 2) for at in (zs - 1 - i, i)]
    for at in order:
        @pl.loop(0, count)
        def _(t, at=at):
            store_coded(x_ref[2 * at + 1 - k, t], ko, kso, at, t)
        for c in side_copies(at):
            c.start()

    def wait_in(pair):
        for c in pair:
            c.wait_recv()

    def pass_on(at, out, out_s, into, into_s, pair, has_more):
        wait_in(side_copies(at))

        @pl.when(has_more)
        def _():
            wait_in(pair)

            @pl.loop(0, count)
            def _(t):
                value = x_ref[2 * at + k, t] + decoded(ki, ksi, at, t) + decoded(into, into_s, at, t)
                store_coded(value, out, out_s, at, t)

        @pl.when(jnp.logical_not(has_more))
        def _():
            @pl.loop(0, count)
            def _(t):
                store_coded(x_ref[2 * at + k, t] + decoded(ki, ksi, at, t), out, out_s, at, t)

        for c in pair:
            c.start()

    for i in range(zs - 1):
        at = zs - 1 - i
        pl.when(z < at)(lambda at=at: pass_on(at, uo, uso, ui, usi, up_copies(at), has_down))
        pl.when(z > i)(lambda i=i: pass_on(i, do, dso, di, dsi, down_copies(i), has_up))

    wait_in(side_copies(z))

    @pl.loop(0, count)
    def _(t):
        o_ref[t] = x_ref[2 * z + k, t] + decoded(ki, ksi, z, t)

    for there, pair, into, into_s in ((has_down, up_copies(z), ui, usi), (has_up, down_copies(z), di, dsi)):
        @pl.when(there)
        def _(pair=pair, into=into, into_s=into_s):
            wait_in(pair)

            @pl.loop(0, count)
            def _(t):
                o_ref[t] += decoded(into, into_s, z, t)

    for at in range(zs):
        for c in side_copies(at):
            c.wait_send()
        for there, pair in ((z < at, up_copies(at)), (z > at, down_copies(at))):
            @pl.when(there)
            def _(pair=pair):
                for c in pair:
                    c.wait_send()
    pl.when(has_left)(lambda: to_left().wait_send())
    pl.when(has_right)(lambda: to_left().wait_recv())


def prep_kernel(size_ref, pick_ref, row_ref, d_ref, m_ref, o_ref):
    count, rows, cols = d_ref.shape
    for f in range(count):
        keep = keep_of(size_ref[f], row_ref[0], (rows, cols))
        m_ref[f] = jnp.where(keep, d_ref[f].astype(jnp.float32), 0.0).astype(m_ref.dtype)
    for s in range(o_ref.shape[0]):
        o_ref[s] = m_ref[pick_ref[s]]


def pack_kernel(src_ref, k_ref, r_ref, o_ref):
    for t in range(o_ref.shape[0]):
        o_ref[t] = r_ref[src_ref[t], :, pl.ds(pl.multiple_of(k_ref[t] * TILE, TILE), TILE)]


def fock_kernel(scale, cls_ref, off_ref, g_ref, l_ref, o_ref, d_scr, acc_scr):
    s = pl.program_id(0)
    lanes, _, slab, _ = g_ref.shape
    basis = l_ref.shape[-1]
    off = off_ref[s]

    @pl.when(s == 0)
    def _():
        o_ref[...] = jnp.zeros_like(o_ref)

    for c in range(1, basis // TILE + 1):
        e = c * TILE

        @pl.when(cls_ref[s] == c)
        def _(c=c, e=e):
            for lane in range(e // slab):
                for k in range(c):
                    d_scr[lane * slab:(lane + 1) * slab, k * TILE:(k + 1) * TILE] = g_ref[lane, off + k]

            for q in range(l_ref.shape[1]):
                lq = l_ref[0, q, :e, :e]
                dm = d_scr[:e, :e]
                prod = jnp.dot(lq, dm, preferred_element_type=jnp.float32).astype(jnp.bfloat16)
                coul = jnp.sum(lq.astype(jnp.float32) * dm.astype(jnp.float32))
                exch = lax.dot_general(
                    prod, lq, (((1,), (1,)), ((), ())), preferred_element_type=jnp.float32
                )
                part = coul * lq.astype(jnp.float32) - 0.5 * exch
                if q == 0:
                    acc_scr[:e, :e] = part
                else:
                    acc_scr[:e, :e] += part
            for lane in range(e // slab):
                for k in range(c):
                    tile = acc_scr[lane * slab:(lane + 1) * slab, k * TILE:(k + 1) * TILE]
                    o_ref[lane, off + k] = (tile * scale).astype(o_ref.dtype)


def unpack_kernel(dst_ref, tile_ref, p_ref, o_ref):
    slots, tiles = tile_ref.shape
    o_ref[...] = jnp.zeros_like(o_ref)
    for s in range(slots):
        for k in range(tiles):
            o_ref[dst_ref[s], :, k * TILE:(k + 1) * TILE] = p_ref[tile_ref[s, k]]


def base_kernel(near_ref, low_ref, mid_ref, high_ref, h_ref, c_ref, o_ref, ext):
    f = pl.program_id(0)
    n = mid_ref.shape[0]

    @pl.when(f == 0)
    def _():
        ext[0:n] = low_ref[...]
        ext[n:2 * n] = mid_ref[...]
        ext[2 * n:3 * n] = high_ref[...]

    total = h_ref[0].astype(jnp.float32)
    for k in range(c_ref.shape[1]):
        total += c_ref[0, k].astype(jnp.float32) * ext[near_ref[f, k]].astype(jnp.float32)
    o_ref[0] = total


def final_kernel(scale, size_ref, slot_ref, row_ref, b_ref, r_ref, o_ref):
    count, rows, cols = b_ref.shape
    for f in range(count):
        keep = keep_of(size_ref[f], row_ref[0], (rows, cols))
        back = r_ref[slot_ref[f]].astype(jnp.float32) * scale
        o_ref[f] = jnp.where(keep, b_ref[f] + back, 0.0)


def local(sizes, neighbors, slot_fragment, density, hcore, integrals, couple):
    i32 = jnp.int32
    groups = lax.axis_size("frag")
    my_group = lax.axis_index("frag")
    core_count = lax.axis_size("ka")
    lanes = lax.axis_size("tile") * core_count
    my_lane = lax.axis_index("tile") * core_count + lax.axis_index("ka")
    per_group, slab, basis = density.shape
    chol_here = integrals.shape[1]
    tiles = basis // TILE
    capacity = max(1, per_group // groups)
    buffers = groups * capacity
    first = my_group * per_group
    ids = jnp.arange(per_group, dtype=i32)
    row0 = (my_lane * slab).astype(i32).reshape(1)
    own_sizes = lax.dynamic_slice_in_dim(sizes, first, per_group)

    bound = 1.5 * (basis * 25 / 32) ** 2 * 6 * 0.15625**2 * chol_here * lanes
    scale = 2.0 ** math.ceil(math.log2(bound / 60000))

    matches = slot_fragment[None, :] == (first + ids)[:, None]
    slot_ids = jnp.arange(slot_fragment.shape[0], dtype=i32)
    slot_of = jnp.sum(jnp.where(matches, slot_ids[None, :], 0), axis=1)
    target = slot_of // per_group
    earlier = ids[None, :] < ids[:, None]
    rank_pos = jnp.sum((target[:, None] == target[None, :]) & earlier, axis=1)
    send_slot = (target * capacity + rank_pos).astype(i32)
    out_ids = jnp.arange(buffers, dtype=i32)
    pick = jnp.sum(jnp.where(out_ids[:, None] == send_slot[None, :], ids[None, :], 0), axis=1).astype(i32)

    held = lax.dynamic_slice_in_dim(slot_fragment, first, per_group)
    source = held // per_group
    before = held[None, :] < held[:, None]
    flat = (source * capacity + jnp.sum((source[:, None] == source[None, :]) & before, axis=1)).astype(i32)

    frag_class = (sizes + TILE - 1) // TILE
    slot_class = jnp.sum(
        jnp.where(slot_fragment[:, None] == slot_ids[None, :], frag_class[None, :], 0), axis=1
    ).astype(i32)
    need = jnp.max(jnp.sum(slot_class.reshape(groups, per_group), axis=1))
    cls = lax.dynamic_slice_in_dim(slot_class, first, per_group)
    off = jnp.sum(jnp.where(earlier, cls[None, :], 0), axis=1).astype(i32)
    most = per_group * tiles
    tile_ids = jnp.arange(most, dtype=i32)
    inside = (tile_ids[:, None] >= off[None, :]) & (tile_ids[:, None] < (off + cls)[None, :])
    tile_src = jnp.sum(jnp.where(inside, flat[None, :], 0), axis=1).astype(i32)
    tile_k = jnp.sum(jnp.where(inside, tile_ids[:, None] - off[None, :], 0), axis=1).astype(i32)
    ks = jnp.arange(tiles, dtype=i32)
    tile_at = jnp.where(ks[None, :] < cls[:, None], off[:, None] + ks[None, :], 0).astype(i32)

    slab_bf = jax.ShapeDtypeStruct((per_group, slab, basis), jnp.bfloat16)
    masked, outgoing = pl.pallas_call(
        prep_kernel,
        out_shape=(slab_bf, jax.ShapeDtypeStruct((buffers, slab, basis), jnp.bfloat16)),
        in_specs=[SM, SM, SM, VM],
        out_specs=(VM, VM),
        name="prep",
    )(own_sizes, pick, row0, density)

    received = lax.all_to_all(
        outgoing.reshape(groups, capacity, slab, basis), "frag", split_axis=0, concat_axis=0, tiled=True
    ).reshape(buffers, slab, basis)

    near = (neighbors - (my_group - 1) * per_group).astype(i32)
    slab_block = (1, slab, basis)
    nnb = couple.shape[1]

    def coupled(low, masked, high, hcore, couple):
        return pl.pallas_call(
            base_kernel,
            grid_spec=pltpu.PrefetchScalarGridSpec(
                num_scalar_prefetch=1,
                grid=(per_group,),
                in_specs=[
                    VM, VM, VM,
                    pl.BlockSpec(slab_block, lambda f, n: (f, 0, 0)),
                    pl.BlockSpec((1, nnb, slab, basis), lambda f, n: (f, 0, 0, 0)),
                ],
                out_specs=pl.BlockSpec(slab_block, lambda f, n: (f, 0, 0)),
                scratch_shapes=[pltpu.VMEM((3 * per_group, slab, basis), jnp.bfloat16)],
            ),
            out_shape=jax.ShapeDtypeStruct((per_group, slab, basis), jnp.float32),
            cost_estimate=pl.CostEstimate(flops=0, bytes_accessed=20 << 20, transcendentals=0),
            name="base",
        )(near, low, masked, high, hcore, couple)

    def branch(ident, count, received, masked, integrals):
        packed = pl.pallas_call(
            pack_kernel,
            out_shape=jax.ShapeDtypeStruct((count, slab, TILE), jnp.bfloat16),
            in_specs=[SM, SM, VM],
            out_specs=VM,
            name="pack",
        )(tile_src, tile_k, received)
        zs = lax.axis_size("tile")
        dma = pltpu.SemaphoreType.DMA
        whole = (lanes, count, slab, TILE)
        gathered, low = pl.pallas_call(
            gather_kernel,
            out_shape=(jax.ShapeDtypeStruct(whole, jnp.bfloat16), slab_bf),
            in_specs=[VM, VM],
            out_specs=(VM, VM),
            scratch_shapes=[dma, dma((zs,)), dma((zs,)), dma((zs,)), dma((zs,)), dma((zs,)), dma, dma],
            compiler_params=pltpu.CompilerParams(
                vmem_limit_bytes=58 << 20, collective_id=2 * ident, has_side_effects=True
            ),
            name="gather",
        )(packed, masked)
        parts = pl.pallas_call(
            partial(fock_kernel, 1.0 / scale),
            grid_spec=pltpu.PrefetchScalarGridSpec(
                num_scalar_prefetch=2,
                grid=(per_group,),
                in_specs=[
                    pl.BlockSpec(whole, lambda s, a, b: (0, 0, 0, 0), pipeline_mode=pl.Buffered(1)),
                    pl.BlockSpec((1, chol_here, basis, basis), lambda s, a, b: (s, 0, 0, 0)),
                ],
                out_specs=pl.BlockSpec(whole, lambda s, a, b: (0, 0, 0, 0)),
                scratch_shapes=[
                    pltpu.VMEM((basis, basis), jnp.bfloat16),
                    pltpu.VMEM((basis, basis), jnp.float32),
                ],
            ),
            out_shape=jax.ShapeDtypeStruct(whole, jnp.float32),
            compiler_params=PAR,
            name="fock",
        )(cls, off, gathered, integrals)
        coded = [
            pltpu.VMEM((zs, count, slab, TILE), jnp.int16),
            pltpu.VMEM((zs, count, TILE), jnp.float32),
        ]
        summed, high = pl.pallas_call(
            reduce_kernel,
            out_shape=(jax.ShapeDtypeStruct((count, slab, TILE), jnp.float32), slab_bf),
            in_specs=[VM, VM],
            out_specs=(VM, VM),
            scratch_shapes=coded * 6 + [dma((2, zs))] * 6 + [dma, dma],
            compiler_params=pltpu.CompilerParams(
                vmem_limit_bytes=58 << 20, collective_id=2 * ident + 1, has_side_effects=True
            ),
            name="reduce",
        )(parts, masked)
        back = pl.pallas_call(
            unpack_kernel,
            out_shape=jax.ShapeDtypeStruct((buffers, slab, basis), jnp.float32),
            in_specs=[SM, SM, VM],
            out_specs=VM,
            name="unpack",
        )(flat, tile_at, summed)
        return back, low, high

    step = max(1, per_group // 4)
    counts = list(range(per_group + 2 * step, most * 5 // 8 + 1, step)) + [most * 3 // 4, most]
    which = jnp.sum(need > jnp.array(counts[:-1], i32)).astype(i32)
    branches = [partial(branch, i, c) for i, c in enumerate(counts)]
    back, low, high = lax.switch(which, branches, received, masked, integrals)
    base = coupled(low, masked, high, hcore, couple)
    returned = lax.all_to_all(
        back.reshape(groups, capacity, slab, basis).astype(WIRE), "frag", split_axis=0, concat_axis=0, tiled=True
    ).reshape(buffers, slab, basis)
    return pl.pallas_call(
        partial(final_kernel, scale),
        out_shape=jax.ShapeDtypeStruct((per_group, slab, basis), jnp.float32),
        in_specs=[SM, SM, SM, VM, VM],
        out_specs=VM,
        name="final",
    )(own_sizes, send_slot, row0, base, returned.astype(jnp.float32))


def solution(mesh):
    return jax.shard_map(
        local,
        mesh=mesh,
        in_specs=(
            P(),
            P("frag", None),
            P(),
            P("frag", ("tile", "ka"), None),
            P("frag", ("tile", "ka"), None),
            P("frag", ("tile", "ka"), None, None),
            P("frag", None, ("tile", "ka"), None),
        ),
        out_specs=P("frag", ("tile", "ka"), None),
        check_vma=False,
    )
```
